32 devices in a mesh: dp: 2 (over core), row: 4 (over y, x), col: 4 (over z).
Axes of the slice: x: 2, y: 2, z: 4, core: 2. Of those that a mesh axis runs over, the one named last changes fastest.
Arguments:
- block_input: bfloat16 [768, 8192], P('row', ('dp', 'col')), may hold values from -6 to 6
- norm_gains: float32 [2, 768], P(None, 'row'), may hold values from 0.1 to 1.9
- row_biases: float32 [4, 768], P(None, 'row'), may hold values from -3 to 3
- w_qkv: bfloat16 [768, 3, 768], P('row', None, 'col'), may hold values from -0.21875 to 0.21875
- qv_bias: float32 [2, 768], P(None, 'col'), may hold values from -3 to 3
- w_out: bfloat16 [768, 768], P('col', 'row'), may hold values from -0.625 to 0.625
- w_up: bfloat16 [768, 3072], P('row', 'col'), may hold values from -0.21875 to 0.21875
- up_bias: float32 [3072], P('col'), may hold values from -3 to 3
- w_down: bfloat16 [768, 3072], P('row', 'col'), may hold values from -0.15625 to 0.15625
- cotangent: bfloat16 [768, 8192], P('row', ('dp', 'col')), may hold values from -6 to 6
Outputs:
- block_output: bfloat16 [768, 8192], P('row', ('dp', 'col'))
- grad_x: bfloat16 [768, 8192], P('row', ('dp', 'col'))
- grad_norm_gains: float32 [2, 768], P(None, 'row')
- grad_row_biases: float32 [4, 768], P(None, 'row')
- grad_w_qkv: float32 [768, 3, 768], P('row', None, 'col')
- grad_qv_bias: float32 [2, 768], P(None, 'col')
- grad_w_out: float32 [768, 768], P('col', 'row')
- grad_w_up: float32 [768, 3072], P('row', 'col')
- grad_up_bias: float32 [3072], P('col')
- grad_w_down: float32 [768, 3072], P('row', 'col')
The draws below stay inside these ranges and needn't reach their ends.
All inputs are finite; a program needn't handle non-finite values.
Results may differ from the reference program's by a relative error of at most 0.013.
Values may be sent and summed in bfloat16 or wider, within the bound.
A program may use at most 192 MiB of HBM per device.

```python
import jax
import jax.numpy as jnp
from jax import lax

D = 768
HEADS = 12
HEAD = 64
FF = 3072
LENGTH = 512
SEQS_DEV = 2
TOKENS = 8192


def block_levels(key, extent, split, low, high):
    def one(dim, shards_of):
        steps = jax.random.uniform(jax.random.fold_in(jax.random.fold_in(key, 6), dim), (shards_of,), jnp.float32, low / len(split), high / len(split))
        return jnp.repeat(jnp.exp(steps), extent[dim] // shards_of).reshape((-1,) + (1,) * (len(extent) - dim - 1))

    loudness = one(*split[0])
    for cut in split[1:]:
        loudness = loudness * one(*cut)
    return loudness


def centred(own_key, extent, scale, bound, cuts=(), dtype=jnp.bfloat16):
    level = block_levels(own_key, extent, cuts, -0.22, 0.18) if cuts else 1.0
    drawn = jax.random.normal(own_key, extent, jnp.float32) * scale * level
    return jnp.minimum(jnp.maximum(drawn, -bound), bound).astype(dtype)


def setup_inputs(seed: int = 0) -> dict:
    splits = jax.random.split(jax.random.key(seed), 11)
    return {
        "block_input": centred(splits[0], (D, TOKENS), 1.0, 6.0, ((0, 4), (1, 8))),
        "norm_gains": jnp.clip(1.0 + 0.18 * jax.random.normal(splits[1], (2, D), jnp.float32), 0.1, 1.9),
        "row_biases": centred(splits[2], (4, D), 0.5, 3.0, ((1, 4),), jnp.float32),
        "w_qkv": centred(splits[3], (D, 3, D), D ** -0.5, 0.21875, ((0, 4), (2, 4))),
        "qv_bias": centred(splits[4], (2, D), 0.5, 3.0, ((1, 4),), jnp.float32),
        "w_out": centred(splits[5], (D, D), (D // 8) ** -0.5, 0.625, ((0, 4), (1, 4))),
        "w_up": centred(splits[6], (D, FF), D ** -0.5, 0.21875, ((0, 4), (1, 4))),
        "up_bias": centred(splits[7], (FF,), 0.5, 3.0, ((0, 4),), jnp.float32),
        "w_down": centred(splits[8], (D, FF), (FF // 2) ** -0.5, 0.15625, ((0, 4), (1, 4))),
        "cotangent": centred(splits[9], (D, TOKENS), 1.0, 6.0, ((0, 4), (1, 8))),
    }


EPSILON = 1e-05
GELU_COEF = 0.7978845608028654

@jax.custom_vjp
def low(v):
    return lax.optimization_barrier(v.astype(jnp.bfloat16)).astype(jnp.float32)

@jax.custom_vjp
def low_back(v):
    return v

def low_keep(v):
    return (low(v), None)

def low_pass(kept, grad):
    return (grad,)

def back_keep(v):
    return (v, None)

def back_low(kept, grad):
    return (low(grad),)
low.defvjp(low_keep, low_pass)
low_back.defvjp(back_keep, back_low)

def matmul(left, right):
    return jnp.dot(left, right, precision=lax.Precision.HIGHEST)

def layer_norm(values, gain, bias):
    center = lax.optimization_barrier(jnp.mean(values, axis=-1, keepdims=True))
    offset = values - center
    spread = lax.optimization_barrier(jnp.mean(offset * offset, axis=-1, keepdims=True))
    return offset * lax.rsqrt(spread + EPSILON) * gain + bias

def gelu_tanh(values):
    return 0.5 * values * (1.0 + jnp.tanh(GELU_COEF * (values + 0.044715 * values * values * values)))

def attend(pieces):
    queries, keys, values = pieces
    scores = jnp.einsum('qhd,khd->hqk', queries, keys, precision=lax.Precision.HIGHEST) * HEAD ** (-0.5)
    scores = low_back(scores)
    positions = jnp.arange(queries.shape[0])
    causal = positions[None, :] <= positions[:, None]
    scores = jnp.where(causal[None], scores, -1e+30)
    summit = lax.optimization_barrier(jnp.max(scores, axis=-1, keepdims=True))
    expos = jnp.exp(scores - summit)
    probs = expos / lax.optimization_barrier(jnp.sum(expos, axis=-1, keepdims=True))
    return jnp.einsum('hqk,khd->qhd', low(probs), values, precision=lax.Precision.HIGHEST)

def forward(block, gains, biases, weight_qkv, bias_qv, weight_out, weight_up, bias_up, weight_down):
    normed = low(layer_norm(block, gains[0], biases[0]))
    mixed = matmul(normed, weight_qkv.reshape(D, 3 * D)).reshape(-1, 3, D)
    bias_three = jnp.stack([bias_qv[0], jnp.zeros_like(bias_qv[0]), bias_qv[1]])
    mixed = low(low_back(mixed + bias_three[None]))
    shaped = (-1, LENGTH, HEADS, HEAD)
    attended = lax.map(jax.checkpoint(attend), (mixed[:, 0].reshape(shaped), mixed[:, 1].reshape(shaped), mixed[:, 2].reshape(shaped)))
    attended = low(low_back(attended.reshape(-1, D)))
    middle = block + low_back(matmul(attended, weight_out) + biases[2])
    normed_two = low(layer_norm(middle, gains[1], biases[1]))
    before = low_back(matmul(normed_two, weight_up) + bias_up)
    hidden = low(gelu_tanh(before))
    return middle + matmul(hidden, weight_down.T) + biases[3]

def reference(block_input, norm_gains, row_biases, w_qkv, qv_bias, w_out, w_up, up_bias, w_down, cotangent):
    params = tuple((arr.astype(jnp.float32) for arr in (norm_gains, row_biases, w_qkv, qv_bias, w_out, w_up, up_bias, w_down)))
    blocks = block_input.astype(jnp.float32).T.reshape(-1, SEQS_DEV * LENGTH, D)
    cots = cotangent.astype(jnp.float32).T.reshape(-1, SEQS_DEV * LENGTH, D)

    def step(totals, pieces):
        block, cot = pieces
        result, pull = jax.vjp(forward, block, *params)
        grads = pull(cot)
        totals = tuple((total + grad for total, grad in zip(totals, grads[1:])))
        return (totals, (result, grads[0]))
    starts = tuple((jnp.zeros_like(param) for param in params))
    totals, (results, input_grads) = lax.scan(step, starts, (blocks, cots))
    return (results.reshape(TOKENS, D).astype(jnp.bfloat16).T, input_grads.reshape(TOKENS, D).astype(jnp.bfloat16).T, totals[0], totals[1], totals[2], totals[3], totals[4], totals[5], totals[6], totals[7])
```

```python
import jax
import jax.numpy as jnp
from jax import lax
from jax.sharding import PartitionSpec as P

D = 768
HEAD = 64
LENGTH = 512


EPSILON = 1e-05
GELU_COEF = 0.7978845608028654


def gelu_tanh(values):
    return (
        0.5 * values * (1.0 + jnp.tanh(GELU_COEF * (values + 0.044715 * values * values * values)))
    )


def multiply(rows, weight, flipped):
    if flipped:
        return lax.dot_general(
            rows, weight, (((1,), (1,)), ((), ())), preferred_element_type=jnp.float32
        )
    return jnp.dot(rows, weight, preferred_element_type=jnp.float32)


def contract_tokens(left, right):
    return lax.dot_general(
        left, right, (((0,), (0,)), ((), ())), preferred_element_type=jnp.float32
    )


def gather(local, axis_name):
    return lax.all_gather(local, axis_name, axis=0, tiled=True)


def scatter_sum(partial, axis_name):
    return lax.psum_scatter(
        partial.astype(jnp.bfloat16), axis_name, scatter_dimension=0, tiled=True
    ).astype(jnp.float32)


def to_tokens(block):
    rows, cols = lax.axis_size("row"), lax.axis_size("col")
    block = lax.all_to_all(block, "row", split_axis=1, concat_axis=0, tiled=True)
    moves = [(r * cols + c, c * rows + r) for r in range(rows) for c in range(cols)]
    return lax.ppermute(block, ("row", "col"), moves).T


def to_features(tokens):
    rows, cols = lax.axis_size("row"), lax.axis_size("col")
    moves = [(c * rows + r, r * cols + c) for r in range(rows) for c in range(cols)]
    block = lax.ppermute(tokens.T, ("row", "col"), moves)
    return lax.all_to_all(block, "row", split_axis=0, concat_axis=1, tiled=True)


def norm_forward(values, gain, bias):
    center = jnp.mean(values, axis=1, keepdims=True)
    offset = values - center
    inverse = lax.rsqrt(jnp.mean(offset * offset, axis=1, keepdims=True) + EPSILON)
    normal = offset * inverse
    return (normal * gain + bias, normal, inverse)


def norm_backward(grad, gain, normal, inverse):
    scaled = grad * gain
    first = jnp.mean(scaled, axis=1, keepdims=True)
    second = jnp.mean(scaled * normal, axis=1, keepdims=True)
    result = inverse * (scaled - first - normal * second)
    return (result, jnp.sum(grad * normal, axis=0), jnp.sum(grad, axis=0))


def causal_mask(length):
    positions = jnp.arange(length)
    return positions[None, :] <= positions[:, None]


def attention_forward(queries, keys, values):
    factor = HEAD ** (-0.5)

    def one_sequence(pieces):
        seq_q, seq_k, seq_v = pieces
        scores = (
            jnp.einsum("qhd,khd->hqk", seq_q, seq_k, preferred_element_type=jnp.float32) * factor
        )
        scores = jnp.where(causal_mask(seq_q.shape[0])[None], scores, -1e30)
        summit = jnp.max(scores, axis=-1, keepdims=True)
        expos = jnp.exp(scores - summit)
        total = jnp.sum(expos, axis=-1, keepdims=True)
        probs = (expos / total).astype(jnp.bfloat16)
        output = jnp.einsum("hqk,khd->qhd", probs, seq_v, preferred_element_type=jnp.float32)
        return (output, summit[..., 0] + jnp.log(total[..., 0]))

    return lax.map(one_sequence, (queries, keys, values))


def attention_backward(queries, keys, values, grad_out, log_sums):
    factor = HEAD ** (-0.5)

    def one_sequence(pieces):
        seq_q, seq_k, seq_v, seq_g, seq_l = pieces
        scores = (
            jnp.einsum("qhd,khd->hqk", seq_q, seq_k, preferred_element_type=jnp.float32) * factor
        )
        scores = jnp.where(causal_mask(seq_q.shape[0])[None], scores, -1e30)
        probs = jnp.exp(scores - seq_l[..., None])
        grad_v = jnp.einsum(
            "hqk,qhd->khd", probs.astype(jnp.bfloat16), seq_g, preferred_element_type=jnp.float32
        )
        grad_p = jnp.einsum("qhd,khd->hqk", seq_g, seq_v, preferred_element_type=jnp.float32)
        inner = jnp.sum(grad_p * probs, axis=-1, keepdims=True)
        grad_s = (probs * (grad_p - inner)).astype(jnp.bfloat16)
        grad_q = (
            jnp.einsum("hqk,khd->qhd", grad_s, seq_k, preferred_element_type=jnp.float32) * factor
        )
        grad_k = (
            jnp.einsum("hqk,qhd->khd", grad_s, seq_q, preferred_element_type=jnp.float32) * factor
        )
        return (grad_q, grad_k, grad_v)

    return lax.map(one_sequence, (queries, keys, values, grad_out, log_sums))


def body(
    block_input, norm_gains, row_biases, w_qkv, qv_bias, w_out, w_up, up_bias, w_down, cotangent
):
    head_cols = w_qkv.shape[2]
    inputs = to_tokens(block_input).astype(jnp.float32)
    cot = to_tokens(cotangent)
    vectors = gather(jnp.concatenate([norm_gains, row_biases], axis=0).T, "row").T
    gains, biases = vectors[:2], vectors[2:]
    qkv_weight = gather(w_qkv.reshape(w_qkv.shape[0], -1), "row")
    rest = gather(jnp.concatenate([w_out.T, w_up, w_down], axis=1), "row")
    width = w_up.shape[1]
    out_t = rest[:, :head_cols]
    up = rest[:, head_cols : head_cols + width]
    down = rest[:, head_cols + width :]

    normed_one, normal_one, inverse_one = norm_forward(inputs, gains[0], biases[0])
    source_one = gather(normed_one.astype(jnp.bfloat16), "col")
    qkv_sum = multiply(source_one, qkv_weight, False)
    rows_here = qkv_sum.shape[0]
    qkv_sum = qkv_sum.reshape(rows_here, 3, head_cols)
    shape_four = (rows_here // LENGTH, LENGTH, head_cols // HEAD, HEAD)
    queries = (qkv_sum[:, 0] + qv_bias[0]).astype(jnp.bfloat16).reshape(shape_four)
    keys_all = qkv_sum[:, 1].astype(jnp.bfloat16).reshape(shape_four)
    values_all = (qkv_sum[:, 2] + qv_bias[1]).astype(jnp.bfloat16).reshape(shape_four)
    attended, log_sums = attention_forward(queries, keys_all, values_all)
    attended_low = attended.reshape(rows_here, head_cols).astype(jnp.bfloat16)
    middle = inputs + scatter_sum(multiply(attended_low, out_t, True), "col") + biases[2]
    normed_two, normal_two, inverse_two = norm_forward(middle, gains[1], biases[1])
    source_two = gather(normed_two.astype(jnp.bfloat16), "col")
    cot_all = gather(cot, "col")
    before = multiply(source_two, up, False) + up_bias
    hidden_low = gelu_tanh(before).astype(jnp.bfloat16)
    grad_hidden = multiply(cot_all, down, False)
    grad_before = jax.vjp(gelu_tanh, before)[1](grad_hidden)[0].astype(jnp.bfloat16)
    grad_normed_two = scatter_sum(multiply(grad_before, up, True), "col")
    output = middle + scatter_sum(multiply(hidden_low, down, True), "col") + biases[3]
    grad_w_down = contract_tokens(cot_all, hidden_low)
    grad_up_bias = jnp.sum(grad_before.astype(jnp.float32), axis=0)
    grad_w_up = contract_tokens(source_two, grad_before)
    grad_out = cot.astype(jnp.float32)
    back_two, gain_two, shift_two = norm_backward(
        grad_normed_two, gains[1], normal_two, inverse_two
    )
    grad_middle = grad_out + back_two
    grad_middle_low = grad_middle.astype(jnp.bfloat16)
    grad_out_bias = jnp.sum(grad_middle_low.astype(jnp.float32), axis=0)
    grad_down_bias = jnp.sum(grad_out, axis=0)
    grad_middle_all = gather(grad_middle_low, "col")
    grad_att_low = multiply(grad_middle_all, out_t, False).astype(jnp.bfloat16).reshape(shape_four)
    grad_w_out_t = contract_tokens(grad_middle_all, attended_low)
    grad_q, grad_k, grad_v = attention_backward(
        queries, keys_all, values_all, grad_att_low, log_sums
    )
    grad_q = grad_q.reshape(rows_here, head_cols).astype(jnp.bfloat16)
    grad_k = grad_k.reshape(rows_here, head_cols).astype(jnp.bfloat16)
    grad_v = grad_v.reshape(rows_here, head_cols).astype(jnp.bfloat16)
    grad_qkv_low = jnp.concatenate([grad_q, grad_k, grad_v], axis=1)
    grad_qv = jnp.stack(
        [jnp.sum(grad_q.astype(jnp.float32), axis=0), jnp.sum(grad_v.astype(jnp.float32), axis=0)]
    )
    grad_normed_one = scatter_sum(multiply(grad_qkv_low, qkv_weight, True), "col")
    grad_w_qkv = contract_tokens(source_one, grad_qkv_low)
    back_one, gain_one, shift_one = norm_backward(
        grad_normed_one, gains[0], normal_one, inverse_one
    )
    grad_input = grad_middle + back_one

    mlp_sum = scatter_sum(
        jnp.concatenate([grad_w_out_t, grad_w_up, grad_w_down], axis=1), "row"
    )
    qkv_grad = scatter_sum(grad_w_qkv, "row")
    weights_sum = lax.psum(
        jnp.concatenate([mlp_sum, qkv_grad], axis=1).astype(jnp.bfloat16), "dp"
    ).astype(jnp.float32)
    sum_out = weights_sum[:, :head_cols].T
    sum_up = weights_sum[:, head_cols : head_cols + width]
    sum_down = weights_sum[:, head_cols + width : head_cols + 2 * width]
    sum_qkv = weights_sum[:, head_cols + 2 * width :].reshape(w_qkv.shape)
    small = jnp.stack([gain_one, gain_two, shift_one, shift_two, grad_out_bias, grad_down_bias])
    small = lax.psum(small, ("dp", "row", "col"))
    share = norm_gains.shape[1]
    small = lax.dynamic_slice_in_dim(small, lax.axis_index("row") * share, share, axis=1)
    sum_qv, sum_upb = lax.psum((grad_qv, grad_up_bias), ("dp", "row"))
    return (
        to_features(output.astype(jnp.bfloat16)),
        to_features(grad_input.astype(jnp.bfloat16)),
        small[:2],
        small[2:],
        sum_qkv,
        sum_qv,
        sum_out,
        sum_up,
        sum_upb,
        sum_down,
    )


def solution(mesh):
    in_specs = (
        P("row", ("dp", "col")),
        P(None, "row"),
        P(None, "row"),
        P("row", None, "col"),
        P(None, "col"),
        P("col", "row"),
        P("row", "col"),
        P("col"),
        P("row", "col"),
        P("row", ("dp", "col")),
    )
    out_specs = (
        P("row", ("dp", "col")),
        P("row", ("dp", "col")),
        P(None, "row"),
        P(None, "row"),
        P("row", None, "col"),
        P(None, "col"),
        P("col", "row"),
        P("row", "col"),
        P("col"),
        P("row", "col"),
    )
    return jax.shard_map(body, mesh=mesh, in_specs=in_specs, out_specs=out_specs, check_vma=False)
```

```python
import functools

import jax
import jax.numpy as jnp
from jax import lax
from jax.experimental import pallas as pl
from jax.experimental.pallas import tpu as pltpu
from jax.sharding import PartitionSpec as P

D = 768
HEAD = 64
LENGTH = 512


EPSILON = 1e-05
GELU_COEF = 0.7978845608028654


def gelu_tanh(values):
    return (
        0.5 * values * (1.0 + jnp.tanh(GELU_COEF * (values + 0.044715 * values * values * values)))
    )


def multiply(rows, weight, flipped):
    if flipped:
        return lax.dot_general(
            rows, weight, (((1,), (1,)), ((), ())), preferred_element_type=jnp.float32
        )
    return jnp.dot(rows, weight, preferred_element_type=jnp.float32)


def contract_tokens(left, right):
    return lax.dot_general(
        left, right, (((0,), (0,)), ((), ())), preferred_element_type=jnp.float32
    )


def swap_kernel(axis_name, count, shared, x_ref, o_ref, send_sem, recv_sem, own_sem):
    me = lax.axis_index(axis_name)
    barrier = pltpu.get_barrier_semaphore()
    peers = [lax.rem(me + step, count) for step in range(1, count)]
    for peer in peers:
        pl.semaphore_signal(
            barrier, inc=1, device_id={axis_name: peer}, device_id_type=pl.DeviceIdType.MESH
        )
    own = pltpu.make_async_copy(x_ref if shared else x_ref.at[me], o_ref.at[me], own_sem)
    own.start()
    pl.semaphore_wait(barrier, count - 1)
    copies = []
    for slot, peer in enumerate(peers):
        copy = pltpu.make_async_remote_copy(
            src_ref=x_ref if shared else x_ref.at[peer],
            dst_ref=o_ref.at[me],
            send_sem=send_sem.at[slot],
            recv_sem=recv_sem.at[slot],
            device_id={axis_name: peer},
            device_id_type=pl.DeviceIdType.MESH,
        )
        copy.start()
        copies.append(copy)
    own.wait()
    for copy in copies:
        copy.wait()


def swap(values, axis_name, shared, ident):
    count = lax.axis_size(axis_name)
    block = values.shape if shared else values.shape[1:]
    moved = values.size * values.dtype.itemsize
    return pl.pallas_call(
        functools.partial(swap_kernel, axis_name, count, shared),
        out_shape=jax.ShapeDtypeStruct((count, *block), values.dtype),
        in_specs=[pl.BlockSpec(memory_space=pltpu.VMEM)],
        out_specs=pl.BlockSpec(memory_space=pltpu.VMEM),
        scratch_shapes=[
            pltpu.SemaphoreType.DMA((count - 1,)),
            pltpu.SemaphoreType.DMA((count - 1,)),
            pltpu.SemaphoreType.DMA,
        ],
        compiler_params=pltpu.CompilerParams(collective_id=ident, has_side_effects=True),
        cost_estimate=pl.CostEstimate(
            flops=0, bytes_accessed=(20 if not shared else 60) * moved, transcendentals=0
        ),
    )(values)


def gather_async(local, axis_name):
    return lax.all_gather(local, axis_name, axis=0, tiled=True)


def scatter_sum_async(partial, axis_name):
    return lax.psum_scatter(
        partial.astype(jnp.bfloat16), axis_name, scatter_dimension=0, tiled=True
    ).astype(jnp.float32)


def gather(local, axis_name, ident):
    return swap(local, axis_name, True, ident).reshape(-1, *local.shape[1:])


def scatter_sum(partial, axis_name, ident):
    count = lax.axis_size(axis_name)
    pieces = partial.astype(jnp.bfloat16).reshape(count, -1, *partial.shape[1:])
    return jnp.sum(swap(pieces, axis_name, False, ident).astype(jnp.float32), axis=0)


def to_tokens(first, second, ident):
    rows, cols = lax.axis_size("row"), lax.axis_size("col")
    share = first.shape[0]
    block = jnp.concatenate([first.T, second.T], axis=1).reshape(rows, -1, 2 * share)
    block = swap(block, "row", False, ident)
    moves = [(r * cols + c, c * rows + r) for r in range(rows) for c in range(cols)]
    block = lax.ppermute(block, ("row", "col"), moves)
    first = jnp.concatenate([block[r, :, :share] for r in range(rows)], axis=1)
    second = jnp.concatenate([block[r, :, share:] for r in range(rows)], axis=1)
    return first, second


def to_features(first, second, ident):
    rows, cols = lax.axis_size("row"), lax.axis_size("col")
    share = first.shape[1] // rows
    block = jnp.stack(
        [
            jnp.concatenate(
                [first[:, r * share : (r + 1) * share], second[:, r * share : (r + 1) * share]], axis=1
            )
            for r in range(rows)
        ]
    )
    moves = [(c * rows + r, r * cols + c) for r in range(rows) for c in range(cols)]
    block = lax.ppermute(block, ("row", "col"), moves)
    block = swap(block, "row", False, ident).reshape(-1, 2 * share)
    return block[:, :share].T, block[:, share:].T


def norm_forward(values, gain, bias):
    center = jnp.mean(values, axis=1, keepdims=True)
    offset = values - center
    inverse = lax.rsqrt(jnp.mean(offset * offset, axis=1, keepdims=True) + EPSILON)
    normal = offset * inverse
    return (normal * gain + bias, normal, inverse)


def norm_backward(grad, gain, normal, inverse):
    scaled = grad * gain
    first = jnp.mean(scaled, axis=1, keepdims=True)
    second = jnp.mean(scaled * normal, axis=1, keepdims=True)
    result = inverse * (scaled - first - normal * second)
    return (result, jnp.sum(grad * normal, axis=0), jnp.sum(grad, axis=0))


def causal_mask(length):
    positions = jnp.arange(length)
    return positions[None, :] <= positions[:, None]


def attention_forward(queries, keys, values):
    factor = HEAD ** (-0.5)

    def one_sequence(pieces):
        seq_q, seq_k, seq_v = pieces
        scores = (
            jnp.einsum("qhd,khd->hqk", seq_q, seq_k, preferred_element_type=jnp.float32) * factor
        )
        scores = jnp.where(causal_mask(seq_q.shape[0])[None], scores, -1e30)
        summit = jnp.max(scores, axis=-1, keepdims=True)
        expos = jnp.exp(scores - summit)
        total = jnp.sum(expos, axis=-1, keepdims=True)
        probs = (expos / total).astype(jnp.bfloat16)
        output = jnp.einsum("hqk,khd->qhd", probs, seq_v, preferred_element_type=jnp.float32)
        return (output, summit[..., 0] + jnp.log(total[..., 0]))

    return lax.map(one_sequence, (queries, keys, values))


def attention_backward(queries, keys, values, grad_out, log_sums):
    factor = HEAD ** (-0.5)

    def one_sequence(pieces):
        seq_q, seq_k, seq_v, seq_g, seq_l = pieces
        scores = (
            jnp.einsum("qhd,khd->hqk", seq_q, seq_k, preferred_element_type=jnp.float32) * factor
        )
        scores = jnp.where(causal_mask(seq_q.shape[0])[None], scores, -1e30)
        probs = jnp.exp(scores - seq_l[..., None])
        grad_v = jnp.einsum(
            "hqk,qhd->khd", probs.astype(jnp.bfloat16), seq_g, preferred_element_type=jnp.float32
        )
        grad_p = jnp.einsum("qhd,khd->hqk", seq_g, seq_v, preferred_element_type=jnp.float32)
        inner = jnp.sum(grad_p * probs, axis=-1, keepdims=True)
        grad_s = (probs * (grad_p - inner)).astype(jnp.bfloat16)
        grad_q = (
            jnp.einsum("hqk,khd->qhd", grad_s, seq_k, preferred_element_type=jnp.float32) * factor
        )
        grad_k = (
            jnp.einsum("hqk,qhd->khd", grad_s, seq_q, preferred_element_type=jnp.float32) * factor
        )
        return (grad_q, grad_k, grad_v)

    return lax.map(one_sequence, (queries, keys, values, grad_out, log_sums))


def body(
    block_input, norm_gains, row_biases, w_qkv, qv_bias, w_out, w_up, up_bias, w_down, cotangent
):
    head_cols = w_qkv.shape[2]
    inputs, cot = to_tokens(block_input, cotangent, 0)
    inputs = inputs.astype(jnp.float32)
    vectors = swap(jnp.concatenate([norm_gains, row_biases], axis=0), "row", True, 1)
    vectors = jnp.concatenate([vectors[r] for r in range(vectors.shape[0])], axis=1)
    gains, biases = vectors[:2], vectors[2:]
    qkv_weight = gather_async(w_qkv.reshape(w_qkv.shape[0], -1), "row")
    rest = gather_async(jnp.concatenate([w_out.T, w_up, w_down], axis=1), "row")
    width = w_up.shape[1]
    out_t = rest[:, :head_cols]
    up = rest[:, head_cols : head_cols + width]
    down = rest[:, head_cols + width :]

    normed_one, normal_one, inverse_one = norm_forward(inputs, gains[0], biases[0])
    source_one = gather(normed_one.astype(jnp.bfloat16), "col", 2)
    qkv_sum = multiply(source_one, qkv_weight, False)
    rows_here = qkv_sum.shape[0]
    qkv_sum = qkv_sum.reshape(rows_here, 3, head_cols)
    shape_four = (rows_here // LENGTH, LENGTH, head_cols // HEAD, HEAD)
    queries = (qkv_sum[:, 0] + qv_bias[0]).astype(jnp.bfloat16).reshape(shape_four)
    keys_all = qkv_sum[:, 1].astype(jnp.bfloat16).reshape(shape_four)
    values_all = (qkv_sum[:, 2] + qv_bias[1]).astype(jnp.bfloat16).reshape(shape_four)
    attended, log_sums = attention_forward(queries, keys_all, values_all)
    attended_low = attended.reshape(rows_here, head_cols).astype(jnp.bfloat16)
    middle = inputs + scatter_sum(multiply(attended_low, out_t, True), "col", 3) + biases[2]
    normed_two, normal_two, inverse_two = norm_forward(middle, gains[1], biases[1])
    source_two = gather(normed_two.astype(jnp.bfloat16), "col", 4)
    cot_all = gather_async(cot, "col")
    before = multiply(source_two, up, False) + up_bias
    hidden_low = gelu_tanh(before).astype(jnp.bfloat16)
    grad_hidden = multiply(cot_all, down, False)
    grad_before = jax.vjp(gelu_tanh, before)[1](grad_hidden)[0].astype(jnp.bfloat16)
    grad_normed_two = scatter_sum(multiply(grad_before, up, True), "col", 5)
    output = middle + scatter_sum_async(multiply(hidden_low, down, True), "col") + biases[3]
    grad_w_down = contract_tokens(cot_all, hidden_low)
    grad_up_bias = jnp.sum(grad_before.astype(jnp.float32), axis=0)
    grad_w_up = contract_tokens(source_two, grad_before)
    grad_out = cot.astype(jnp.float32)
    back_two, gain_two, shift_two = norm_backward(
        grad_normed_two, gains[1], normal_two, inverse_two
    )
    grad_middle = grad_out + back_two
    grad_middle_low = grad_middle.astype(jnp.bfloat16)
    grad_out_bias = jnp.sum(grad_middle_low.astype(jnp.float32), axis=0)
    grad_down_bias = jnp.sum(grad_out, axis=0)
    grad_middle_all = gather(grad_middle_low, "col", 6)
    grad_att_low = multiply(grad_middle_all, out_t, False).astype(jnp.bfloat16).reshape(shape_four)
    grad_w_out_t = contract_tokens(grad_middle_all, attended_low)
    grad_q, grad_k, grad_v = attention_backward(
        queries, keys_all, values_all, grad_att_low, log_sums
    )
    grad_q = grad_q.reshape(rows_here, head_cols).astype(jnp.bfloat16)
    grad_k = grad_k.reshape(rows_here, head_cols).astype(jnp.bfloat16)
    grad_v = grad_v.reshape(rows_here, head_cols).astype(jnp.bfloat16)
    grad_qkv_low = jnp.concatenate([grad_q, grad_k, grad_v], axis=1)
    grad_qv = jnp.stack(
        [jnp.sum(grad_q.astype(jnp.float32), axis=0), jnp.sum(grad_v.astype(jnp.float32), axis=0)]
    )
    grad_normed_one = scatter_sum(multiply(grad_qkv_low, qkv_weight, True), "col", 7)
    grad_w_qkv = contract_tokens(source_one, grad_qkv_low)
    back_one, gain_one, shift_one = norm_backward(
        grad_normed_one, gains[0], normal_one, inverse_one
    )
    grad_input = grad_middle + back_one

    mlp_sum = scatter_sum_async(jnp.concatenate([grad_w_up, grad_w_down], axis=1), "row")
    mlp_sum = lax.psum(mlp_sum.astype(jnp.bfloat16), "dp").astype(jnp.float32)
    att_sum = scatter_sum(jnp.concatenate([grad_w_qkv, grad_w_out_t], axis=1), "row", 8)
    att_sum = jnp.sum(
        swap(att_sum.astype(jnp.bfloat16), "dp", True, 9).astype(jnp.float32), axis=0
    )
    sum_up = mlp_sum[:, :width]
    sum_down = mlp_sum[:, width:]
    sum_qkv = att_sum[:, : 3 * head_cols].reshape(w_qkv.shape)
    sum_out = att_sum[:, 3 * head_cols :].T
    features = gains.shape[1]
    longest = max(features, width, 2 * head_cols)
    small = [gain_one, gain_two, shift_one, shift_two, grad_out_bias, grad_down_bias]
    small = small + [grad_up_bias, grad_qv.reshape(-1)]
    small = jnp.stack([jnp.pad(row, (0, longest - row.shape[0])) for row in small])
    small = jnp.sum(swap(small, "dp", True, 10), axis=0)
    small = jnp.sum(swap(small, "row", True, 11), axis=0)
    sum_upb = small[6, :width]
    sum_qv = small[7, : 2 * head_cols].reshape(2, head_cols)
    share = norm_gains.shape[1]
    small = lax.dynamic_slice_in_dim(small[:6], lax.axis_index("row") * share, share, axis=1)
    small = jnp.sum(swap(small, "col", True, 12), axis=0)
    output_t, grad_input_t = to_features(
        output.astype(jnp.bfloat16), grad_input.astype(jnp.bfloat16), 13
    )
    return (
        output_t,
        grad_input_t,
        small[:2],
        small[2:],
        sum_qkv,
        sum_qv,
        sum_out,
        sum_up,
        sum_upb,
        sum_down,
    )


def solution(mesh):
    in_specs = (
        P("row", ("dp", "col")),
        P(None, "row"),
        P(None, "row"),
        P("row", None, "col"),
        P(None, "col"),
        P("col", "row"),
        P("row", "col"),
        P("col"),
        P("row", "col"),
        P("row", ("dp", "col")),
    )
    out_specs = (
        P("row", ("dp", "col")),
        P("row", ("dp", "col")),
        P(None, "row"),
        P(None, "row"),
        P("row", None, "col"),
        P(None, "col"),
        P("col", "row"),
        P("row", "col"),
        P("col"),
        P("row", "col"),
    )
    return jax.shard_map(body, mesh=mesh, in_specs=in_specs, out_specs=out_specs, check_vma=False)
```

```python
import functools

import jax
import jax.numpy as jnp
from jax import lax
from jax.experimental import pallas as pl
from jax.experimental.pallas import tpu as pltpu
from jax.sharding import PartitionSpec as P

D = 768
HEAD = 64
LENGTH = 512


EPSILON = 1e-05
GELU_COEF = 0.7978845608028654


def gelu_tanh(values):
    return (
        0.5 * values * (1.0 + jnp.tanh(GELU_COEF * (values + 0.044715 * values * values * values)))
    )


def multiply(rows, weight, flipped):
    if flipped:
        return lax.dot_general(
            rows, weight, (((1,), (1,)), ((), ())), preferred_element_type=jnp.float32
        )
    return jnp.dot(rows, weight, preferred_element_type=jnp.float32)


def contract_tokens(left, right):
    return lax.dot_general(
        left, right, (((0,), (0,)), ((), ())), preferred_element_type=jnp.float32
    )


def swap_kernel(axis_name, count, shared, x_ref, o_ref, send_sem, recv_sem, own_sem):
    me = lax.axis_index(axis_name)
    barrier = pltpu.get_barrier_semaphore()
    peers = [lax.rem(me + step, count) for step in range(1, count)]
    for peer in peers:
        pl.semaphore_signal(
            barrier, inc=1, device_id={axis_name: peer}, device_id_type=pl.DeviceIdType.MESH
        )
    own = pltpu.make_async_copy(x_ref if shared else x_ref.at[me], o_ref.at[me], own_sem)
    own.start()
    pl.semaphore_wait(barrier, count - 1)
    copies = []
    for slot, peer in enumerate(peers):
        copy = pltpu.make_async_remote_copy(
            src_ref=x_ref if shared else x_ref.at[peer],
            dst_ref=o_ref.at[me],
            send_sem=send_sem.at[slot],
            recv_sem=recv_sem.at[slot],
            device_id={axis_name: peer},
            device_id_type=pl.DeviceIdType.MESH,
        )
        copy.start()
        copies.append(copy)
    own.wait()
    for copy in copies:
        copy.wait()


def swap(values, axis_name, shared, ident):
    count = lax.axis_size(axis_name)
    block = values.shape if shared else values.shape[1:]
    moved = values.size * values.dtype.itemsize
    return pl.pallas_call(
        functools.partial(swap_kernel, axis_name, count, shared),
        out_shape=jax.ShapeDtypeStruct((count, *block), values.dtype),
        in_specs=[pl.BlockSpec(memory_space=pltpu.VMEM)],
        out_specs=pl.BlockSpec(memory_space=pltpu.VMEM),
        scratch_shapes=[
            pltpu.SemaphoreType.DMA((count - 1,)),
            pltpu.SemaphoreType.DMA((count - 1,)),
            pltpu.SemaphoreType.DMA,
        ],
        compiler_params=pltpu.CompilerParams(collective_id=ident, has_side_effects=True),
        cost_estimate=pl.CostEstimate(
            flops=0, bytes_accessed=(20 if not shared else 60) * moved, transcendentals=0
        ),
    )(values)


def gather_async(local, axis_name):
    return lax.all_gather(local, axis_name, axis=0, tiled=True)


def scatter_sum_async(partial, axis_name):
    return lax.psum_scatter(
        partial.astype(jnp.bfloat16), axis_name, scatter_dimension=0, tiled=True
    ).astype(jnp.float32)


def gather(local, axis_name, ident):
    return swap(local, axis_name, True, ident).reshape(-1, *local.shape[1:])


def scatter_sum(partial, axis_name, ident):
    count = lax.axis_size(axis_name)
    pieces = partial.astype(jnp.bfloat16).reshape(count, -1, *partial.shape[1:])
    return jnp.sum(swap(pieces, axis_name, False, ident).astype(jnp.float32), axis=0)


def to_tokens(first, second, ident):
    rows, cols = lax.axis_size("row"), lax.axis_size("col")
    share = first.shape[0]
    block = jnp.concatenate([first.T, second.T], axis=1).reshape(rows, -1, 2 * share)
    block = swap(block, "row", False, ident)
    if rows != cols:
        moves = [(r * cols + c, c * rows + r) for r in range(rows) for c in range(cols)]
        block = lax.ppermute(block, ("row", "col"), moves)
    first = jnp.concatenate([block[r, :, :share] for r in range(rows)], axis=1)
    second = jnp.concatenate([block[r, :, share:] for r in range(rows)], axis=1)
    return first, second


def to_features(first, second, ident):
    rows, cols = lax.axis_size("row"), lax.axis_size("col")
    share = first.shape[1] // rows
    block = jnp.stack(
        [
            jnp.concatenate(
                [first[:, r * share : (r + 1) * share], second[:, r * share : (r + 1) * share]], axis=1
            )
            for r in range(rows)
        ]
    )
    if rows != cols:
        moves = [(c * rows + r, r * cols + c) for r in range(rows) for c in range(cols)]
        block = lax.ppermute(block, ("row", "col"), moves)
    block = swap(block, "row", False, ident).reshape(-1, 2 * share)
    return block[:, :share].T, block[:, share:].T


def flip(block):
    rows, cols = lax.axis_size("row"), lax.axis_size("col")
    if rows != cols:
        return block
    moves = [(r * cols + c, c * rows + r) for r in range(rows) for c in range(cols)]
    return lax.ppermute(block, ("row", "col"), moves)


def norm_forward(values, gain, bias):
    center = jnp.mean(values, axis=1, keepdims=True)
    offset = values - center
    inverse = lax.rsqrt(jnp.mean(offset * offset, axis=1, keepdims=True) + EPSILON)
    normal = offset * inverse
    return (normal * gain + bias, normal, inverse)


def norm_backward(grad, gain, normal, inverse):
    scaled = grad * gain
    first = jnp.mean(scaled, axis=1, keepdims=True)
    second = jnp.mean(scaled * normal, axis=1, keepdims=True)
    result = inverse * (scaled - first - normal * second)
    return (result, jnp.sum(grad * normal, axis=0), jnp.sum(grad, axis=0))


def causal_mask(length):
    positions = jnp.arange(length)
    return positions[None, :] <= positions[:, None]


def attention_forward(queries, keys, values):
    factor = HEAD ** (-0.5)

    def one_sequence(pieces):
        seq_q, seq_k, seq_v = pieces
        scores = (
            jnp.einsum("qhd,khd->hqk", seq_q, seq_k, preferred_element_type=jnp.float32) * factor
        )
        scores = jnp.where(causal_mask(seq_q.shape[0])[None], scores, -1e30)
        summit = jnp.max(scores, axis=-1, keepdims=True)
        expos = jnp.exp(scores - summit)
        total = jnp.sum(expos, axis=-1, keepdims=True)
        probs = (expos / total).astype(jnp.bfloat16)
        output = jnp.einsum("hqk,khd->qhd", probs, seq_v, preferred_element_type=jnp.float32)
        return (output, summit[..., 0] + jnp.log(total[..., 0]))

    return lax.map(one_sequence, (queries, keys, values))


def attention_backward(queries, keys, values, grad_out, log_sums):
    factor = HEAD ** (-0.5)

    def one_sequence(pieces):
        seq_q, seq_k, seq_v, seq_g, seq_l = pieces
        scores = (
            jnp.einsum("qhd,khd->hqk", seq_q, seq_k, preferred_element_type=jnp.float32) * factor
        )
        scores = jnp.where(causal_mask(seq_q.shape[0])[None], scores, -1e30)
        probs = jnp.exp(scores - seq_l[..., None])
        grad_v = jnp.einsum(
            "hqk,qhd->khd", probs.astype(jnp.bfloat16), seq_g, preferred_element_type=jnp.float32
        )
        grad_p = jnp.einsum("qhd,khd->hqk", seq_g, seq_v, preferred_element_type=jnp.float32)
        inner = jnp.sum(grad_p * probs, axis=-1, keepdims=True)
        grad_s = (probs * (grad_p - inner)).astype(jnp.bfloat16)
        grad_q = (
            jnp.einsum("hqk,khd->qhd", grad_s, seq_k, preferred_element_type=jnp.float32) * factor
        )
        grad_k = (
            jnp.einsum("hqk,qhd->khd", grad_s, seq_q, preferred_element_type=jnp.float32) * factor
        )
        return (grad_q, grad_k, grad_v)

    return lax.map(one_sequence, (queries, keys, values, grad_out, log_sums))


def body(
    block_input, norm_gains, row_biases, w_qkv, qv_bias, w_out, w_up, up_bias, w_down, cotangent
):
    head_cols = w_qkv.shape[2]
    square = lax.axis_size("row") == lax.axis_size("col")
    heads_axis, split_axis = ("row", "col") if square else ("col", "row")
    qv_bias, up_bias = flip(qv_bias), flip(up_bias)
    inputs, cot = to_tokens(block_input, cotangent, 0)
    inputs = inputs.astype(jnp.float32)
    vectors = swap(jnp.concatenate([norm_gains, row_biases], axis=0), "row", True, 1)
    vectors = jnp.concatenate([vectors[r] for r in range(vectors.shape[0])], axis=1)
    gains, biases = vectors[:2], vectors[2:]
    qkv_weight = gather_async(flip(w_qkv.reshape(w_qkv.shape[0], -1)), split_axis)
    rest = gather_async(flip(jnp.concatenate([w_out.T, w_up, w_down], axis=1)), split_axis)
    width = w_up.shape[1]
    out_t = rest[:, :head_cols]
    up = rest[:, head_cols : head_cols + width]
    down = rest[:, head_cols + width :]

    normed_one, normal_one, inverse_one = norm_forward(inputs, gains[0], biases[0])
    source_one = gather(normed_one.astype(jnp.bfloat16), heads_axis, 2)
    qkv_sum = multiply(source_one, qkv_weight, False)
    rows_here = qkv_sum.shape[0]
    qkv_sum = qkv_sum.reshape(rows_here, 3, head_cols)
    shape_four = (rows_here // LENGTH, LENGTH, head_cols // HEAD, HEAD)
    queries = (qkv_sum[:, 0] + qv_bias[0]).astype(jnp.bfloat16).reshape(shape_four)
    keys_all = qkv_sum[:, 1].astype(jnp.bfloat16).reshape(shape_four)
    values_all = (qkv_sum[:, 2] + qv_bias[1]).astype(jnp.bfloat16).reshape(shape_four)
    attended, log_sums = attention_forward(queries, keys_all, values_all)
    attended_low = attended.reshape(rows_here, head_cols).astype(jnp.bfloat16)
    middle = inputs + scatter_sum(multiply(attended_low, out_t, True), heads_axis, 3) + biases[2]
    normed_two, normal_two, inverse_two = norm_forward(middle, gains[1], biases[1])
    source_two = gather(normed_two.astype(jnp.bfloat16), heads_axis, 4)
    cot_all = gather_async(cot, heads_axis)
    before = multiply(source_two, up, False) + up_bias
    hidden_low = gelu_tanh(before).astype(jnp.bfloat16)
    grad_hidden = multiply(cot_all, down, False)
    grad_before = jax.vjp(gelu_tanh, before)[1](grad_hidden)[0].astype(jnp.bfloat16)
    grad_normed_two = scatter_sum(multiply(grad_before, up, True), heads_axis, 5)
    output = middle + scatter_sum_async(multiply(hidden_low, down, True), heads_axis) + biases[3]
    grad_w_down = contract_tokens(cot_all, hidden_low)
    grad_up_bias = jnp.sum(grad_before.astype(jnp.float32), axis=0)
    grad_w_up = contract_tokens(source_two, grad_before)
    grad_out = cot.astype(jnp.float32)
    back_two, gain_two, shift_two = norm_backward(
        grad_normed_two, gains[1], normal_two, inverse_two
    )
    grad_middle = grad_out + back_two
    grad_middle_low = grad_middle.astype(jnp.bfloat16)
    grad_out_bias = jnp.sum(grad_middle_low.astype(jnp.float32), axis=0)
    grad_down_bias = jnp.sum(grad_out, axis=0)
    grad_middle_all = gather(grad_middle_low, heads_axis, 6)
    grad_att_low = multiply(grad_middle_all, out_t, False).astype(jnp.bfloat16).reshape(shape_four)
    grad_w_out_t = contract_tokens(grad_middle_all, attended_low)
    grad_q, grad_k, grad_v = attention_backward(
        queries, keys_all, values_all, grad_att_low, log_sums
    )
    grad_q = grad_q.reshape(rows_here, head_cols).astype(jnp.bfloat16)
    grad_k = grad_k.reshape(rows_here, head_cols).astype(jnp.bfloat16)
    grad_v = grad_v.reshape(rows_here, head_cols).astype(jnp.bfloat16)
    grad_qkv_low = jnp.concatenate([grad_q, grad_k, grad_v], axis=1)
    grad_qv = jnp.stack(
        [jnp.sum(grad_q.astype(jnp.float32), axis=0), jnp.sum(grad_v.astype(jnp.float32), axis=0)]
    )
    grad_normed_one = scatter_sum(multiply(grad_qkv_low, qkv_weight, True), heads_axis, 7)
    grad_w_qkv = contract_tokens(source_one, grad_qkv_low)
    back_one, gain_one, shift_one = norm_backward(
        grad_normed_one, gains[0], normal_one, inverse_one
    )
    grad_input = grad_middle + back_one

    mlp_sum = scatter_sum_async(jnp.concatenate([grad_w_up, grad_w_down], axis=1), split_axis)
    mlp_sum = flip(lax.psum(mlp_sum.astype(jnp.bfloat16), "dp")).astype(jnp.float32)
    att_sum = scatter_sum(jnp.concatenate([grad_w_qkv, grad_w_out_t], axis=1), split_axis, 8)
    att_sum = jnp.sum(
        swap(flip(att_sum.astype(jnp.bfloat16)), "dp", True, 9).astype(jnp.float32), axis=0
    )
    sum_up = mlp_sum[:, :width]
    sum_down = mlp_sum[:, width:]
    sum_qkv = att_sum[:, : 3 * head_cols].reshape(w_qkv.shape)
    sum_out = att_sum[:, 3 * head_cols :].T
    features = gains.shape[1]
    longest = max(features, width, 2 * head_cols)
    small = [gain_one, gain_two, shift_one, shift_two, grad_out_bias, grad_down_bias]
    small = small + [grad_up_bias, grad_qv.reshape(-1)]
    small = jnp.stack([jnp.pad(row, (0, longest - row.shape[0])) for row in small])
    small = jnp.sum(swap(small, "dp", True, 10), axis=0)
    small = jnp.sum(swap(small, split_axis, True, 11), axis=0)
    projected = flip(small[6:])
    sum_upb = projected[0, :width]
    sum_qv = projected[1, : 2 * head_cols].reshape(2, head_cols)
    share = norm_gains.shape[1]
    small = jnp.sum(swap(small[:6], heads_axis, True, 12), axis=0)
    small = lax.dynamic_slice_in_dim(small, lax.axis_index("row") * share, share, axis=1)
    output_t, grad_input_t = to_features(
        output.astype(jnp.bfloat16), grad_input.astype(jnp.bfloat16), 13
    )
    return (
        output_t,
        grad_input_t,
        small[:2],
        small[2:],
        sum_qkv,
        sum_qv,
        sum_out,
        sum_up,
        sum_upb,
        sum_down,
    )


def solution(mesh):
    in_specs = (
        P("row", ("dp", "col")),
        P(None, "row"),
        P(None, "row"),
        P("row", None, "col"),
        P(None, "col"),
        P("col", "row"),
        P("row", "col"),
        P("col"),
        P("row", "col"),
        P("row", ("dp", "col")),
    )
    out_specs = (
        P("row", ("dp", "col")),
        P("row", ("dp", "col")),
        P(None, "row"),
        P(None, "row"),
        P("row", None, "col"),
        P(None, "col"),
        P("col", "row"),
        P("row", "col"),
        P("col"),
        P("row", "col"),
    )
    return jax.shard_map(body, mesh=mesh, in_specs=in_specs, out_specs=out_specs, check_vma=False)
```
